128 devices in a mesh: dp: 128 (over x, z, y, core).
Axes of the slice: x: 4, y: 4, z: 4, core: 2. Of those that a mesh axis runs over, the one named last changes fastest.
Arguments:
- step_index: int32 [1], replicated, may hold values from 0 to 63
- dest: int32 [2, 32768, 1], P(None, 'dp'), may hold values from 0 to 127; in each aligned block of 256 rows (0 to 255, 256 to 511, ..., all dimensions but the last counted through in order) at most 4 rows name the same one
- tokens: bfloat16 [2, 32768, 1024], P(None, 'dp'), may hold values from -6 to 6
- params: float32 [131072, 1024], P('dp'), may hold values from -0.1875 to 0.1875
- trackers: float32 [131072, 1024], P('dp'), may hold values from -4 to 4
- old_grads: float32 [131072, 1024], P('dp'), may hold values from -4 to 4
- key_weight: bfloat16 [1024, 1024], replicated, may hold values from -0.1875 to 0.1875
- latents: bfloat16 [128, 1024], replicated, may hold values from -6 to 6
- targets: float32 [16384, 1024], P('dp'), may hold values from -6 to 6
Outputs:
- new_params: float32 [131072, 1024], P('dp')
- new_trackers: float32 [131072, 1024], P('dp')
The draws below stay inside these ranges and needn't reach their ends.
Inputs may be any that keep to these rules, and one draw needn't show every extreme that they name: `dest`: in each step no trainer receives more than 4 rows from the rows of one device, and that bound is reached; every trainer receives some row.
All inputs are finite; a program needn't handle non-finite values.
Results may differ from the reference program's by a relative error of at most 0.012.
Values may be sent and summed in bfloat16 or wider, within the bound.
A program may use at most 128 MiB of HBM per device.

```python
import math
import jax
import jax.numpy as jnp
import numpy as np
from jax import lax

D = 1024
HEADS = 16
HEAD_DIM = 64
LAT = 128
ROWS_DEV = 256
STEPS = 2
CAP = 4
WINDOW = 512
TOKENS = 32768
N_DP = 128


def levels(own_key, extent, shards, least, largest):
    def one(position, parts):
        steps = jax.random.uniform(jax.random.fold_in(jax.random.fold_in(own_key, 6), position), (parts,), jnp.float32, least / len(shards), largest / len(shards))
        return jnp.repeat(jnp.exp(steps), extent[position] // parts).reshape((-1,) + (1,) * (len(extent) - position - 1))

    gain = one(*shards[0])
    for cut in shards[1:]:
        gain = gain * one(*cut)
    return gain


def routed_block(rng, own, number, rows, number_of, top, limit, lean):
    ranking = jax.random.permutation(rng, number_of)
    packed, ordinary = shares(number_of, rows * top, limit, lean, True), shares(number_of, rows * top, limit, lean, False)
    places = jnp.arange(number_of)

    def named(lengths, offset_by):
        used = int((lengths > 0).sum())
        fixed = max(1, used // 4)
        moved = fixed + (places - fixed + offset_by * (used - fixed)) % max(1, number_of - fixed)
        return jnp.zeros((number_of,), jnp.int32).at[ranking[jnp.where(places < fixed, places, moved)]].set(jnp.asarray(lengths, jnp.int32))

    lengths = jnp.where(number % 4 == 0, named(packed, number // 4), named(ordinary, number - number // 4 - 1))
    mixed = jax.random.permutation(jax.random.fold_in(own, 3), number_of)
    donor, receiver = mixed[0:number_of // 2 * 2:2], mixed[1:number_of // 2 * 2:2]
    margin = jnp.minimum(lengths[donor] - 1, limit - lengths[receiver]) // 2
    margin = jnp.where((donor == ranking[0]) | (receiver == ranking[0]) | (lengths[receiver] == 0), 0, jnp.maximum(margin, 0))
    moved = jax.random.randint(jax.random.fold_in(own, 4), (number_of // 2,), 0, 1 << 20) % (margin + 1)
    lengths = lengths.at[donor].add(-moved).at[receiver].add(moved)
    items = jnp.searchsorted(jnp.cumsum(lengths), jnp.arange(rows * top), side="right").astype(jnp.int32)
    listing = items.reshape(top, rows).T
    listing = listing[jax.random.permutation(jax.random.fold_in(own, 1), rows)]
    offset_by = jax.random.randint(jax.random.fold_in(own, 2), (rows, 1), 0, top)
    return jnp.take_along_axis(listing, (jnp.arange(top)[None, :] + offset_by) % top, axis=1)


def shares(amount, total, limit, slope, full):
    weights = [(1 << 20) // math.isqrt(grade ** slope) + 1 for grade in range(1, amount + 1)]
    largest = limit if full else min(limit, max(-(-total // amount), total * weights[0] // sum(weights)))
    least = 1 if total - largest >= amount - 1 else 0
    holding, surplus = [largest] + [least] * (amount - 1), total - largest - least * (amount - 1)
    while surplus > 0:
        candidates = [i for i in range(1, amount) if holding[i] < largest] or [i for i in range(1, amount) if holding[i] < limit]
        pool, remaining = sum([weights[i] for i in candidates]), surplus
        for i in candidates:
            more = min(limit - holding[i], max(1, remaining * weights[i] // pool), surplus)
            holding[i] = holding[i] + more
            surplus = surplus - more
    return np.array(holding)


def scatter_about(stream_key, shape, deviation, limit, cuts=(), kind=jnp.bfloat16):
    result = deviation * jax.random.normal(stream_key, shape, jnp.float32)
    if cuts:
        result = result * levels(stream_key, shape, cuts, -0.22, 0.18)
    return jnp.clip(result, -limit, limit).astype(kind)


def setup_inputs(seed: int = 0) -> dict:
    arg_keys = jax.random.split(jax.random.key(seed), 10)
    step_index = jax.random.randint(arg_keys[0], (1,), 0, 64).astype(jnp.int32)
    dest_keys = jax.random.split(jax.random.fold_in(arg_keys[1], 1), STEPS * TOKENS // ROWS_DEV)
    dest_turns = jax.random.permutation(jax.random.fold_in(arg_keys[1], 3), STEPS * TOKENS // ROWS_DEV)
    dest = jax.vmap(lambda own, number: routed_block(jax.random.fold_in(arg_keys[1], 2), own, number, ROWS_DEV, N_DP, 1, CAP, 2))(dest_keys, dest_turns).reshape((STEPS, TOKENS, 1))
    tokens = scatter_about(arg_keys[2], (STEPS, TOKENS, D), 1.0, 6.0, ((1, 128),))
    params = scatter_about(arg_keys[3], (N_DP * D, D), D ** -0.5, 0.1875, ((0, 128),), jnp.float32)
    trackers = scatter_about(arg_keys[4], (N_DP * D, D), 0.5, 4.0, ((0, 128),), jnp.float32)
    old_grads = scatter_about(arg_keys[5], (N_DP * D, D), 0.5, 4.0, ((0, 128),), jnp.float32)
    key_weight = scatter_about(arg_keys[6], (D, D), D ** -0.5, 0.1875)
    latents = scatter_about(arg_keys[7], (LAT, D), 1.0, 6.0)
    targets = scatter_about(arg_keys[8], (N_DP * LAT, D), 1.0, 6.0, ((0, 128),), jnp.float32)
    return {"step_index": step_index, "dest": dest, "tokens": tokens, "params": params, "trackers": trackers, "old_grads": old_grads, "key_weight": key_weight, "latents": latents, "targets": targets}


def local_grad(weight, rows, live, key_weight, latents, target):
    win = rows.shape[0]
    keys = jnp.dot(rows, key_weight, preferred_element_type=jnp.float32).astype(jnp.bfloat16)
    values = jnp.dot(rows, weight.astype(jnp.bfloat16), preferred_element_type=jnp.float32).astype(jnp.bfloat16)
    queries = latents.astype(jnp.float32).reshape(LAT, HEADS, HEAD_DIM)
    keyed = keys.astype(jnp.float32).reshape(win, HEADS, HEAD_DIM)
    scores = jnp.einsum('lhd,jhd->hlj', queries, keyed) / jnp.sqrt(jnp.float32(HEAD_DIM))
    attn = (jax.nn.sigmoid(scores - 3.5) * live[None, None, :]).astype(jnp.bfloat16)
    attf = attn.astype(jnp.float32)
    out = jnp.einsum('hlj,jhd->lhd', attf, values.astype(jnp.float32).reshape(win, HEADS, HEAD_DIM)).reshape(LAT, D)
    resid = ((out - target) / 16.0).astype(jnp.bfloat16)
    dvalues = jnp.einsum('hlj,lhd->jhd', attf, resid.astype(jnp.float32).reshape(LAT, HEADS, HEAD_DIM))
    dvalues = dvalues.reshape(win, D).astype(jnp.bfloat16)
    return lax.dot_general(rows, dvalues, (((0,), (0,)), ((), ())), preferred_element_type=jnp.float32)

def reference(step_index, dest, tokens, params, trackers, old_grads, key_weight, latents, targets):
    logn = int(N_DP).bit_length() - 1
    params_all = params.reshape(N_DP, D, D)
    track_all = trackers.reshape(N_DP, D, D)
    grads_all = old_grads.reshape(N_DP, D, D)
    target_all = targets.reshape(N_DP, LAT, D)
    trainer_ids = jnp.arange(N_DP, dtype=jnp.int32)
    for step in range(STEPS):
        bit = (step_index[0] + step) % logn
        partner = jnp.bitwise_xor(trainer_ids, jnp.left_shift(jnp.int32(1), bit.astype(jnp.int32))).astype(jnp.int32)
        new_params = 0.5 * (params_all + params_all[partner]) - 0.05 * track_all
        mixed_track = 0.5 * (track_all + track_all[partner])
        owner = dest[step, :, 0]
        order = jnp.argsort(owner, stable=True)
        sorted_rows = jnp.concatenate([tokens[step][order], jnp.zeros((WINDOW, D), jnp.bfloat16)], axis=0)
        counts = lax.optimization_barrier(jnp.sum((owner[:, None] == trainer_ids[None, :]).astype(jnp.int32), axis=0))
        starts = (jnp.cumsum(counts) - counts).astype(jnp.int32)

        def one(idx):
            rows = lax.dynamic_slice(sorted_rows, (starts[idx], jnp.int32(0)), (WINDOW, D))
            live = (jnp.arange(WINDOW, dtype=jnp.int32) < counts[idx]).astype(jnp.float32)
            return local_grad(new_params[idx], rows, live, key_weight, latents, target_all[idx])
        new_grads = lax.map(one, trainer_ids)
        track_all = mixed_track + new_grads - grads_all
        grads_all = new_grads
        params_all = new_params
    return (params_all.reshape(N_DP * D, D), track_all.reshape(N_DP * D, D))
```

```python
from functools import partial

import jax
import jax.numpy as jnp
from jax import lax
from jax.experimental import pallas as pl
from jax.experimental.pallas import tpu as pltpu
from jax.sharding import PartitionSpec as P

HEADS = 16
STEPS = 2
CAP = 4
CHUNKS = 8
MESH = pl.DeviceIdType.MESH
F32 = jnp.float32
BF16 = jnp.bfloat16


def axis_of(bit):
    return 0 if bit == 0 else 1 + (bit - 1) // 2


def tracking_kernel(
    b0, b1,
    x_hbm, y_hbm, g_hbm, r1_hbm, r2_hbm, kw_hbm, lat_hbm, tgt_hbm,
    ox_hbm, oy_hbm,
    x_v, y_v, g_v, xs, ys, xr, yr, x1s, x1r, y1s, y1r, w2,
    rows1, rows2, kw, lat, tgt, keys, att, att_t, att2, att2_t, acc, vals, dv,
    in_sem, small_sem, out_sem, xss, xrs, yss, yrs, x1ss, x1rs, y1ss, y1rs,
):
    me = lax.axis_index("dp")
    size = x_v.shape[0] // CHUNKS
    width = x_v.shape[1]
    pairs = width // 128
    shared = axis_of(b0) == axis_of(b1)

    def flip(where, bit):
        step = 2**bit
        return where + step * (1 - 2 * ((where // step) % 2))

    p1 = flip(me, b0)
    p2 = flip(me, b1)
    px = flip(p1, b1) if shared else p2
    peers = (p1, p2, px) if shared else (p1, p2)

    def part(ref, c):
        return ref.at[pl.ds(pl.multiple_of(c * size, size), size)]

    def send(src, dst, ss, rs, c, peer):
        return pltpu.make_async_remote_copy(
            src_ref=part(src, c), dst_ref=part(dst, c), send_sem=ss.at[c], recv_sem=rs.at[c],
            device_id=(peer,), device_id_type=MESH)

    def fetch(src, dst, k, c):
        return pltpu.make_async_copy(part(src, c), part(dst, c), in_sem.at[k, c])

    def put(src, dst, k, c):
        return pltpu.make_async_copy(part(src, c), part(dst, c), out_sem.at[k, c])

    def each(body):
        lax.fori_loop(0, CHUNKS, lambda c, carry: (body(c), carry)[1], 0)

    smalls = [pltpu.make_async_copy(a, b, small_sem.at[k]) for k, (a, b) in enumerate(
        ((r1_hbm, rows1), (kw_hbm, kw), (lat_hbm, lat), (r2_hbm, rows2), (tgt_hbm, tgt)))]

    each(lambda c: fetch(x_hbm, x_v, 0, c).start())
    each(lambda c: fetch(y_hbm, y_v, 1, c).start())
    for copy in smalls:
        copy.start()
    each(lambda c: fetch(g_hbm, g_v, 2, c).start())

    barrier = pltpu.get_barrier_semaphore()
    for peer in peers:
        pl.semaphore_signal(barrier, inc=1, device_id=(peer,), device_id_type=MESH)
    pl.semaphore_wait(barrier, len(peers))

    def first(c):
        fetch(x_hbm, x_v, 0, c).wait()
        part(xs, c)[...] = part(x_v, c)[...].astype(BF16)
        send(xs, xr, xss, xrs, c, p1).start()

    each(first)

    def second(c):
        fetch(y_hbm, y_v, 1, c).wait()
        part(ys, c)[...] = part(y_v, c)[...].astype(BF16)
        send(ys, yr, yss, yrs, c, p1).start()

    each(second)
    for copy in smalls:
        copy.wait()

    low = lax.broadcasted_iota(jnp.int32, (128, 128), 1) < 64
    zero = jnp.zeros((128, 128), BF16)

    def lanes(p, wide=128):
        return pl.ds(pl.multiple_of(p * wide, wide), wide)

    def stacked(block):
        return jnp.concatenate([jnp.where(low, block, zero), jnp.where(low, zero, block)], axis=0)

    def make_keys(rows):
        def body(p, carry):
            keys[:, lanes(p, 256)] = jnp.dot(
                rows[...], kw[:, lanes(p, 256)], preferred_element_type=F32).astype(BF16)
            return carry
        lax.fori_loop(0, width // 256, body, 0)

    def attend(p, a, a_t):
        query = stacked(lat[:, lanes(p)])
        key = keys[:, lanes(p)]
        over = (((1,), (1,)), ((), ()))
        score = lax.dot_general(query, key, over, preferred_element_type=F32)
        a[p] = jax.nn.sigmoid(score * 0.125 - 3.5).astype(BF16)
        score = lax.dot_general(key, query, over, preferred_element_type=F32)
        a_t[p] = jax.nn.sigmoid(score * 0.125 - 3.5).astype(BF16)

    def accumulate(rows, weight, c):
        acc[...] += jnp.dot(rows[:, lanes(c)], part(weight, c)[...], preferred_element_type=F32)

    def residuals(a, a_t):
        vals[...] = acc[...].astype(BF16)

        def body(p, carry):
            both = jnp.dot(a[p], vals[:, lanes(p)], preferred_element_type=F32)
            out = jnp.where(low, both[:128], both[128:])
            resid = ((out - tgt[:, lanes(p)]) * 0.0625).astype(BF16)
            dv[:, lanes(p)] = jnp.dot(a_t[p], stacked(resid), preferred_element_type=F32).astype(BF16)
            return carry
        lax.fori_loop(0, pairs, body, 0)

    def grad(rows, c):
        return lax.dot_general(
            rows[:, lanes(c)], dv[...], (((0,), (0,)), ((), ())), preferred_element_type=F32)

    make_keys(rows1)
    acc[...] = jnp.zeros_like(acc)

    def third(c):
        attend(c, att, att_t)
        send(xs, xr, xss, xrs, c, p1).wait_recv()
        x1 = 0.5 * (part(x_v, c)[...] + part(xr, c)[...].astype(F32)) - 0.05 * part(y_v, c)[...]
        part(x_v, c)[...] = x1
        part(x1s, c)[...] = x1.astype(BF16)
        accumulate(rows1, x1s, c)
        if not shared:
            send(x1s, x1r, x1ss, x1rs, c, px).start()

    each(third)
    residuals(att, att_t)
    make_keys(rows2)
    acc[...] = jnp.zeros_like(acc)

    def mix(c):
        send(x1s, x1r, x1ss, x1rs, c, px).wait_recv()
        x2 = 0.5 * (part(x_v, c)[...] + part(x1r, c)[...].astype(F32)) - 0.05 * part(y_v, c)[...]
        part(x_v, c)[...] = x2
        part(w2, c)[...] = x2.astype(BF16)
        accumulate(rows2, w2, c)
        put(x_v, ox_hbm, 0, c).start()

    def fourth(c):
        attend(c, att2, att2_t)
        fetch(g_hbm, g_v, 2, c).wait()
        g1 = grad(rows1, c)
        send(ys, yr, yss, yrs, c, p1).wait_recv()
        mine = part(y_v, c)[...]
        other = part(yr, c)[...].astype(F32)
        if shared:
            part(w2, c)[...] = (part(x_v, c)[...] + 0.05 * (mine - other)).astype(BF16)
        y1 = 0.5 * (mine + other) + g1 - part(g_v, c)[...]
        part(y_v, c)[...] = y1
        part(g_v, c)[...] = 0.5 * y1 - g1
        part(y1s, c)[...] = y1.astype(BF16)
        if shared:
            send(w2, x1r, x1ss, x1rs, c, px).start()
        send(y1s, y1r, y1ss, y1rs, c, p2).start()
        if not shared:
            mix(c)

    each(fourth)
    if shared:
        def later(c):
            send(w2, x1r, x1ss, x1rs, c, px).wait_send()
            mix(c)
        each(later)
    residuals(att2, att2_t)

    def last(c):
        g2 = grad(rows2, c)
        send(y1s, y1r, y1ss, y1rs, c, p2).wait_recv()
        part(g_v, c)[...] = part(g_v, c)[...] + 0.5 * part(y1r, c)[...].astype(F32) + g2
        put(g_v, oy_hbm, 1, c).start()

    each(last)

    def drain(c):
        send(xs, xr, xss, xrs, c, p1).wait_send()
        send(ys, yr, yss, yrs, c, p1).wait_send()
        send(y1s, y1r, y1ss, y1rs, c, p2).wait_send()
        if not shared:
            send(x1s, x1r, x1ss, x1rs, c, px).wait_send()
        put(x_v, ox_hbm, 0, c).wait()
        put(g_v, oy_hbm, 1, c).wait()

    each(drain)


def track(b0, b1, params, trackers, old_grads, rows1, rows2, key_weight, latents, targets):
    tall, width = params.shape
    win, count_lat = rows1.shape[0], latents.shape[0]
    pairs = width // 128
    half = pltpu.VMEM((tall, width), BF16)
    full = pltpu.VMEM((tall, width), F32)
    chunked = pltpu.SemaphoreType.DMA((CHUNKS,))
    hbm = pl.BlockSpec(memory_space=pl.ANY)
    return pl.pallas_call(
        partial(tracking_kernel, b0, b1),
        out_shape=(jax.ShapeDtypeStruct(params.shape, F32), jax.ShapeDtypeStruct(params.shape, F32)),
        in_specs=[hbm] * 8,
        out_specs=(hbm, hbm),
        scratch_shapes=[full] * 3 + [half] * 9 + [
            pltpu.VMEM((win, width), BF16), pltpu.VMEM((win, width), BF16),
            pltpu.VMEM((width, width), BF16), pltpu.VMEM((count_lat, width), BF16),
            pltpu.VMEM((count_lat, width), F32), pltpu.VMEM((win, width), BF16),
            pltpu.VMEM((pairs, 2 * count_lat, win), BF16), pltpu.VMEM((pairs, win, 2 * count_lat), BF16),
            pltpu.VMEM((pairs, 2 * count_lat, win), BF16), pltpu.VMEM((pairs, win, 2 * count_lat), BF16),
            pltpu.VMEM((win, width), F32), pltpu.VMEM((win, width), BF16), pltpu.VMEM((win, width), BF16),
            pltpu.SemaphoreType.DMA((3, CHUNKS)), pltpu.SemaphoreType.DMA((5,)), pltpu.SemaphoreType.DMA((2, CHUNKS)),
        ] + [chunked] * 8,
        name="tracking",
        compiler_params=pltpu.CompilerParams(
            collective_id=1 + b0, has_side_effects=True, vmem_limit_bytes=60 * 2**20),
    )(params, trackers, old_grads, rows1, rows2, key_weight, latents, targets)


def pack_rows(owner, token_rows, count_dev):
    rows = token_rows.shape[0]
    onehot = (owner[:, None] == jnp.arange(count_dev, dtype=jnp.int32)[None, :]).astype(BF16)
    order = jnp.arange(rows)
    before = (order[:, None] > order[None, :]).astype(BF16)
    counts = jnp.dot(before, onehot, preferred_element_type=F32)
    rank = jnp.sum(counts * onehot.astype(F32), axis=1).astype(jnp.int32)
    where = owner * CAP + rank
    slots = jnp.arange(count_dev * CAP, dtype=jnp.int32)
    place = (slots[:, None] == where[None, :]).astype(BF16)
    return jnp.dot(place, token_rows, preferred_element_type=F32).astype(BF16)


def shards(step_index, dest, tokens, params, trackers, old_grads, key_weight, latents, targets):
    count_dev = lax.axis_size("dp")
    logn = count_dev.bit_length() - 1
    width = tokens.shape[2]
    rows = []
    for step in range(STEPS):
        packed = pack_rows(dest[step, :, 0], tokens[step], count_dev).reshape(count_dev, CAP, width)
        rows.append(lax.all_to_all(packed, "dp", split_axis=0, concat_axis=0, tiled=True).reshape(-1, width))
    return lax.switch(
        step_index[0] % logn,
        [partial(track, bit, (bit + 1) % logn) for bit in range(logn)],
        params, trackers, old_grads, rows[0], rows[1], key_weight, latents, targets)


def solution(mesh):
    in_specs = (
        P(),
        P(None, "dp", None),
        P(None, "dp", None),
        P("dp", None),
        P("dp", None),
        P("dp", None),
        P(),
        P(),
        P("dp", None),
    )
    out_specs = (P("dp", None), P("dp", None))
    return jax.shard_map(shards, mesh=mesh, in_specs=in_specs, out_specs=out_specs, check_vma=False)
```

```python
from functools import partial

import jax
import jax.numpy as jnp
from jax import lax
from jax.experimental import pallas as pl
from jax.experimental.pallas import tpu as pltpu
from jax.sharding import PartitionSpec as P

HEADS = 16
STEPS = 2
CAP = 4
CHUNKS = 8
LEAD = 2
MESH = pl.DeviceIdType.MESH
F32 = jnp.float32
BF16 = jnp.bfloat16


def axis_of(bit):
    return 0 if bit == 0 else 1 + (bit - 1) // 2


def tracking_kernel(
    b0, b1,
    dest_hbm, tok_hbm, x_hbm, y_hbm, g_hbm, kw_hbm, lat_hbm, tgt_hbm,
    ox_hbm, oy_hbm,
    x_v, y_v, g_v, xs, ys, xr, yr, x1s, x1r, y1s, y1r, w2,
    dest, tok, mail, got, rows1, rows2, kw, lat, tgt, att, att_t, att2, att2_t, acc, vals, dv,
    in_sem, small_sem, out_sem, own_sem, xss, xrs, yss, yrs, x1ss, x1rs, y1ss, y1rs, mss, mrs,
):
    me = lax.axis_index("dp")
    count_dev = mail.shape[0]
    size = x_v.shape[0] // CHUNKS
    width = x_v.shape[1]
    pairs = width // 128
    shared = axis_of(b0) == axis_of(b1)

    def flip(where, bit):
        step = 2**bit
        return where + step * (1 - 2 * ((where // step) % 2))

    p1 = flip(me, b0)
    p2 = flip(me, b1)
    px = flip(p1, b1) if shared else p2

    def part(ref, c):
        return ref.at[pl.ds(pl.multiple_of(c * size, size), size)]

    def send(src, dst, ss, rs, c, peer):
        return pltpu.make_async_remote_copy(
            src_ref=part(src, c), dst_ref=part(dst, c), send_sem=ss.at[c], recv_sem=rs.at[c],
            device_id=(peer,), device_id_type=MESH)

    def fetch(src, dst, k, c):
        return pltpu.make_async_copy(part(src, c), part(dst, c), in_sem.at[k, c])

    def put(src, dst, k, c):
        return pltpu.make_async_copy(part(src, c), part(dst, c), out_sem.at[k, c])

    def each(body, start=0, stop=CHUNKS):
        lax.fori_loop(start, stop, lambda c, carry: (body(c), carry)[1], 0)

    smalls = [pltpu.make_async_copy(a, b, small_sem.at[k]) for k, (a, b) in enumerate(
        ((dest_hbm, dest), (tok_hbm, tok), (kw_hbm, kw), (lat_hbm, lat), (tgt_hbm, tgt)))]

    barrier = pltpu.get_barrier_semaphore()

    def greet(k):
        pl.semaphore_signal(barrier, inc=1, device_id=((me + k) % count_dev,), device_id_type=MESH)

    each(lambda c: fetch(x_hbm, x_v, 0, c).start(), 0, LEAD)
    smalls[0].start()
    smalls[1].start()
    each(lambda c: fetch(x_hbm, x_v, 0, c).start(), LEAD)
    each(greet, 1, count_dev)
    each(lambda c: fetch(y_hbm, y_v, 1, c).start())
    for copy in smalls[2:]:
        copy.start()
    each(lambda c: fetch(g_hbm, g_v, 2, c).start())

    def mail_to(k):
        peer = (me + k) % count_dev
        return pltpu.make_async_remote_copy(
            src_ref=mail.at[peer], dst_ref=got.at[me], send_sem=mss.at[k], recv_sem=mrs.at[k],
            device_id=(peer,), device_id_type=MESH)

    def mail_from(k):
        source = (me + count_dev - k) % count_dev
        return pltpu.make_async_remote_copy(
            src_ref=mail.at[source], dst_ref=got.at[source], send_sem=mss.at[k], recv_sem=mrs.at[k],
            device_id=(source,), device_id_type=MESH)

    own = pltpu.make_async_copy(mail.at[me], got.at[me], own_sem)

    def pack(step):
        rows = tok.shape[1]
        across = jnp.broadcast_to(dest[step:step + 1, :], (rows, rows)).astype(F32)
        down = across.T
        earlier = lax.broadcasted_iota(jnp.int32, (rows, rows), 0) < lax.broadcasted_iota(
            jnp.int32, (rows, rows), 1)
        rank = jnp.sum(jnp.where(earlier & (across == down), 1.0, 0.0), axis=0, keepdims=True)
        where = across[:1] * CAP + rank
        block = 256

        def body(n, carry):
            index = lax.broadcasted_iota(jnp.int32, (block, 1), 0)
            slot = (n * (block // 8) + index // 8) * CAP + index % CAP
            place = (slot.astype(F32) == where).astype(BF16)
            half = tok.shape[2] // 2
            left = jnp.dot(place, tok[step, :, :half], preferred_element_type=F32)
            right = jnp.dot(place, tok[step, :, half:], preferred_element_type=F32)
            piece = jnp.where(index % 8 < CAP, left, right).astype(BF16)
            mail[pl.ds(n * (block // 8), block // 8), 8 * step:8 * step + 8, :] = piece.reshape(block // 8, 8, half)
            return carry

        lax.fori_loop(0, count_dev * 8 // block, body, 0)

    def unpack():
        block = 16

        def body(n, carry):
            half = got.shape[2]
            top = got[pl.ds(n * block, block)].astype(F32).reshape(block, 2, 8, half)
            bottom = got[pl.ds(count_dev // 2 + n * block, block)].astype(F32).reshape(block, 2, 8, half)
            for step, rows in enumerate((rows1, rows2)):
                a = top[:, step].reshape(block * 8, half)
                b = bottom[:, step].reshape(block * 8, half)
                upper = lax.broadcasted_iota(jnp.int32, (block * 8, half), 0) % 8 < CAP
                place = pl.ds(pl.multiple_of(n * block * 8, block * 8), block * 8)
                rows[place, :half] = jnp.where(upper, a, pltpu.roll(b, CAP, 0)).astype(BF16)
                rows[place, half:] = jnp.where(upper, pltpu.roll(a, block * 8 - CAP, 0), b).astype(BF16)
            return carry

        lax.fori_loop(0, count_dev // 2 // block, body, 0)

    def first(c):
        fetch(x_hbm, x_v, 0, c).wait()
        part(xs, c)[...] = part(x_v, c)[...].astype(BF16)
        send(xs, xr, xss, xrs, c, p1).start()

    smalls[0].wait()
    smalls[1].wait()
    pl.semaphore_wait(barrier, count_dev - 1)
    each(first, 0, LEAD)
    pack(0)
    pack(1)
    own.start()
    each(lambda k: mail_to(k).start(), 1, count_dev)
    each(first, LEAD)

    def second(c):
        fetch(y_hbm, y_v, 1, c).wait()
        part(ys, c)[...] = part(y_v, c)[...].astype(BF16)
        send(ys, yr, yss, yrs, c, p1).start()

    each(second)
    for copy in smalls[2:]:
        copy.wait()

    low = lax.broadcasted_iota(jnp.int32, (128, 128), 1) < 64
    zero = jnp.zeros((128, 128), BF16)

    def lanes(p, wide=128):
        return pl.ds(pl.multiple_of(p * wide, wide), wide)

    def stacked(block):
        return jnp.concatenate([jnp.where(low, block, zero), jnp.where(low, zero, block)], axis=0)

    def attend(rows, p, a, a_t):
        query = stacked(lat[:, lanes(p)])
        key = jnp.dot(rows[...], kw[:, lanes(p)], preferred_element_type=F32).astype(BF16)
        over = (((1,), (1,)), ((), ()))
        score = lax.dot_general(query, key, over, preferred_element_type=F32)
        a[p] = jax.nn.sigmoid(score * 0.125 - 3.5).astype(BF16)
        score = lax.dot_general(key, query, over, preferred_element_type=F32)
        a_t[p] = jax.nn.sigmoid(score * 0.125 - 3.5).astype(BF16)

    def accumulate(rows, weight, c):
        acc[...] += jnp.dot(rows[:, lanes(c)], part(weight, c)[...], preferred_element_type=F32)

    def residuals(a, a_t):
        vals[...] = acc[...].astype(BF16)

        def body(p, carry):
            both = jnp.dot(a[p], vals[:, lanes(p)], preferred_element_type=F32)
            out = jnp.where(low, both[:128], both[128:])
            resid = ((out - tgt[:, lanes(p)]) * 0.0625).astype(BF16)
            dv[:, lanes(p)] = jnp.dot(a_t[p], stacked(resid), preferred_element_type=F32).astype(BF16)
            return carry
        lax.fori_loop(0, pairs, body, 0)

    def grad(rows, c):
        return lax.dot_general(
            rows[:, lanes(c)], dv[...], (((0,), (0,)), ((), ())), preferred_element_type=F32)

    def third(c):
        send(xs, xr, xss, xrs, c, p1).wait_recv()
        x1 = 0.5 * (part(x_v, c)[...] + part(xr, c)[...].astype(F32)) - 0.05 * part(y_v, c)[...]
        part(x_v, c)[...] = x1
        part(x1s, c)[...] = x1.astype(BF16)
        if not shared:
            send(x1s, x1r, x1ss, x1rs, c, px).start()

    each(third, 0, LEAD)
    own.wait()
    each(lambda k: mail_from(k).wait_recv(), 1, count_dev)
    unpack()
    acc[...] = jnp.zeros_like(acc)

    def lead(c):
        attend(rows1, c, att, att_t)
        accumulate(rows1, x1s, c)

    each(lead, 0, LEAD)

    def rest(c):
        attend(rows1, c, att, att_t)
        third(c)
        accumulate(rows1, x1s, c)

    each(rest, LEAD)
    residuals(att, att_t)
    acc[...] = jnp.zeros_like(acc)

    def mix(c):
        send(x1s, x1r, x1ss, x1rs, c, px).wait_recv()
        x2 = 0.5 * (part(x_v, c)[...] + part(x1r, c)[...].astype(F32)) - 0.05 * part(y_v, c)[...]
        part(x_v, c)[...] = x2
        part(w2, c)[...] = x2.astype(BF16)
        accumulate(rows2, w2, c)
        put(x_v, ox_hbm, 0, c).start()

    def fourth(c):
        attend(rows2, c, att2, att2_t)
        fetch(g_hbm, g_v, 2, c).wait()
        g1 = grad(rows1, c)
        send(ys, yr, yss, yrs, c, p1).wait_recv()
        mine = part(y_v, c)[...]
        other = part(yr, c)[...].astype(F32)
        if shared:
            part(w2, c)[...] = (part(x_v, c)[...] + 0.05 * (mine - other)).astype(BF16)
        y1 = 0.5 * (mine + other) + g1 - part(g_v, c)[...]
        part(y_v, c)[...] = y1
        part(g_v, c)[...] = 0.5 * y1 - g1
        part(y1s, c)[...] = y1.astype(BF16)
        if shared:
            send(w2, x1r, x1ss, x1rs, c, px).start()
        send(y1s, y1r, y1ss, y1rs, c, p2).start()
        if not shared:
            mix(c)

    each(fourth)
    if shared:
        def later(c):
            send(w2, x1r, x1ss, x1rs, c, px).wait_send()
            mix(c)
        each(later)
    residuals(att2, att2_t)

    def last(c):
        g2 = grad(rows2, c)
        send(y1s, y1r, y1ss, y1rs, c, p2).wait_recv()
        part(g_v, c)[...] = part(g_v, c)[...] + 0.5 * part(y1r, c)[...].astype(F32) + g2
        put(g_v, oy_hbm, 1, c).start()

    each(last)

    def drain(c):
        send(xs, xr, xss, xrs, c, p1).wait_send()
        send(ys, yr, yss, yrs, c, p1).wait_send()
        send(y1s, y1r, y1ss, y1rs, c, p2).wait_send()
        if not shared:
            send(x1s, x1r, x1ss, x1rs, c, px).wait_send()
        put(x_v, ox_hbm, 0, c).wait()
        put(g_v, oy_hbm, 1, c).wait()

    each(drain)
    each(lambda k: mail_to(k).wait_send(), 1, count_dev)


def track(b0, b1, dest, tokens, params, trackers, old_grads, key_weight, latents, targets):
    tall, width = params.shape
    count_dev, count_lat = lax.axis_size("dp"), latents.shape[0]
    win = count_dev * CAP
    pairs = width // 128
    half = pltpu.VMEM((tall, width), BF16)
    full = pltpu.VMEM((tall, width), F32)
    chunked = pltpu.SemaphoreType.DMA((CHUNKS,))
    mails = pltpu.VMEM((count_dev, 16, width // 2), BF16)
    hbm = pl.BlockSpec(memory_space=pl.ANY)
    return pl.pallas_call(
        partial(tracking_kernel, b0, b1),
        out_shape=(jax.ShapeDtypeStruct(params.shape, F32), jax.ShapeDtypeStruct(params.shape, F32)),
        in_specs=[hbm] * 8,
        out_specs=(hbm, hbm),
        scratch_shapes=[full] * 3 + [half] * 9 + [
            pltpu.VMEM(dest.shape, jnp.int32), pltpu.VMEM(tokens.shape, BF16), mails, mails,
            pltpu.VMEM((win, width), BF16), pltpu.VMEM((win, width), BF16),
            pltpu.VMEM((width, width), BF16), pltpu.VMEM((count_lat, width), BF16),
            pltpu.VMEM((count_lat, width), F32),
            pltpu.VMEM((pairs, 2 * count_lat, win), BF16), pltpu.VMEM((pairs, win, 2 * count_lat), BF16),
            pltpu.VMEM((pairs, 2 * count_lat, win), BF16), pltpu.VMEM((pairs, win, 2 * count_lat), BF16),
            pltpu.VMEM((win, width), F32), pltpu.VMEM((win, width), BF16), pltpu.VMEM((win, width), BF16),
            pltpu.SemaphoreType.DMA((3, CHUNKS)), pltpu.SemaphoreType.DMA((5,)), pltpu.SemaphoreType.DMA((2, CHUNKS)),
            pltpu.SemaphoreType.DMA,
        ] + [chunked] * 8 + [pltpu.SemaphoreType.DMA((count_dev,))] * 2,
        name="tracking",
        compiler_params=pltpu.CompilerParams(
            collective_id=1 + b0, has_side_effects=True, vmem_limit_bytes=60 * 2**20),
    )(dest, tokens, params, trackers, old_grads, key_weight, latents, targets)


def shards(step_index, dest, tokens, params, trackers, old_grads, key_weight, latents, targets):
    logn = lax.axis_size("dp").bit_length() - 1
    return lax.switch(
        step_index[0] % logn,
        [partial(track, bit, (bit + 1) % logn) for bit in range(logn)],
        dest[:, :, 0], tokens, params, trackers, old_grads, key_weight, latents, targets)


def solution(mesh):
    in_specs = (
        P(),
        P(None, "dp", None),
        P(None, "dp", None),
        P("dp", None),
        P("dp", None),
        P("dp", None),
        P(),
        P(),
        P("dp", None),
    )
    out_specs = (P("dp", None), P("dp", None))
    return jax.shard_map(shards, mesh=mesh, in_specs=in_specs, out_specs=out_specs, check_vma=False)
```
